32 devices in a mesh: ctx: 8 (over z, y), head: 4 (over x, core).
Axes of the slice: x: 2, y: 2, z: 4, core: 2. Of those that a mesh axis runs over, the one named last changes fastest.
Arguments:
- queries: bfloat16 [4096, 4096], P('ctx', 'head'), may hold values from -40 to 40
- key_rows: bfloat16 [4096, 1024], P('ctx', 'head'), may hold values from -10 to 10
- value_rows: bfloat16 [4096, 1024], P('ctx', 'head'), may hold values from -6 to 6
- cotangent: bfloat16 [4096, 4096], P('ctx', 'head'), may hold values from -6 to 6
- equation_lengths: int32 [8], replicated, may hold values from 1 to 2048, 4096 in all
Outputs:
- attention: bfloat16 [4096, 4096], P(('ctx', 'head'))
- query_grad: bfloat16 [4096, 4096], P(('ctx', 'head'))
- key_grad: bfloat16 [4096, 1024], P(('ctx', 'head'))
- value_grad: bfloat16 [4096, 1024], P(('ctx', 'head'))
The draws below stay inside these ranges and needn't reach their ends.
Inputs may be any that keep to these rules, and one draw needn't show every extreme that they name: `equation_lengths`: the equations fill the sequence in order; the longest has exactly 2048 tokens.
All inputs are finite; a program needn't handle non-finite values.
Results may differ from the reference program's by a relative error of at most 0.012.
Values may be sent and summed in bfloat16 or wider, within the bound.
No kernel may reach another device: no remote copies, remote signals or barrier semaphores. Data moves between devices by JAX's collectives and lax.ppermute only.
A program may use at most 128 MiB of HBM per device.

```python
import math
import jax
import jax.numpy as jnp
import numpy as np
from jax import lax

HEADS = 32
KVH = 8
HD = 128
TOK_DEV = 512
MOST = 2048
REACH = 4
SEQ = 4096
DOCS = 8


def draw_queries(key, part):
    drawn = jnp.clip(jax.random.normal(jax.random.fold_in(key, 11), (SEQ, HEADS * HD), jnp.float32), -6.0, 6.0)
    return drawn.astype(jnp.bfloat16)


def draw_key_rows(key, part):
    drawn = jnp.clip(jax.random.normal(jax.random.fold_in(key, 12), (SEQ, KVH * HD), jnp.float32), -6.0, 6.0)
    return drawn.astype(jnp.bfloat16)


def levels(key, extent, pieces, smallest, largest):
    factor_of = 1.0
    for dim, shards_of in pieces:
        heights = jax.random.uniform(jax.random.fold_in(jax.random.fold_in(key, 6), dim), (shards_of,), jnp.float32, smallest / len(pieces), largest / len(pieces))
        factor_of = factor_of * jnp.repeat(jnp.exp(heights), extent[dim] // shards_of).reshape((-1,) + (1,) * (len(extent) - 1 - dim))
    return factor_of


def profile(amount, total, limit, slope):
    weights = [(1 << 20) // math.isqrt(rank ** slope) + 1 for rank in range(2, amount + 1)]
    spare, holding = total - limit - (amount - 1), [1] * (amount - 1)
    while spare > 0:
        free = [i for i in range(amount - 1) if holding[i] < limit]
        whole, remaining = sum([weights[i] for i in free]), spare
        for i in free:
            more = min(limit - holding[i], max(1, remaining * weights[i] // whole), spare)
            holding[i] = holding[i] + more
            spare = spare - more
    return np.array([limit] + holding)


def ragged(key, amount, total, reach, slope):
    if amount == 2:
        one = jax.random.randint(key, (), max(1, total - reach), min(reach, total - 1) + 1)
        return jnp.stack([one, total - one])
    tallies = jnp.asarray(profile(amount, total, reach, slope), jnp.int32)
    couples = (amount - 1) // 2
    donor, sink = tallies[1:1 + 2 * couples:2], tallies[2:2 + 2 * couples:2]
    room = jnp.minimum(donor - 1, reach - sink)
    shifted = jax.random.randint(jax.random.fold_in(key, 1), (couples,), 0, 1 << 20) % (room + 1)
    tallies = tallies.at[1:1 + 2 * couples:2].set(donor - shifted).at[2:2 + 2 * couples:2].set(sink + shifted)
    return tallies[jax.random.permutation(jax.random.fold_in(key, 2), amount)]


def noise(rng, shape, scale, limit, shards=(), held_as=jnp.bfloat16):
    loudness = levels(rng, shape, shards, -0.22, 0.18) if shards else 1.0
    array = jax.random.normal(rng, shape, jnp.float32) * scale * loudness
    return jnp.minimum(jnp.maximum(array, -limit), limit).astype(held_as)


def setup_inputs(seed: int = 0) -> dict:
    key_list = jax.random.split(jax.random.key(seed), 6)
    queries = draw_queries(jax.random.fold_in(key_list[5], 71), 0)
    key_rows = draw_key_rows(jax.random.fold_in(key_list[5], 71), 0)
    value_rows = noise(key_list[2], (SEQ, KVH * HD), 1.0, 6.0, ((0, 8), (1, 4)))
    cotangent = noise(key_list[3], (SEQ, HEADS * HD), 1.0, 6.0, ((0, 8), (1, 4)))
    equation_lengths = ragged(key_list[4], DOCS, SEQ, MOST, 2).astype(jnp.int32)
    return {"queries": queries, "key_rows": key_rows, "value_rows": value_rows, "cotangent": cotangent, "equation_lengths": equation_lengths}


def equation_ids(starts, positions):
    return jnp.sum((starts[None, :] <= positions[:, None]).astype(jnp.int32), axis=1) - 1


def reference(queries, key_rows, value_rows, cotangent, equation_lengths):
    seq_len = queries.shape[0]
    block_len = TOK_DEV
    window = (REACH + 1) * block_len
    pad_len = REACH * block_len
    block_count = seq_len // block_len
    kv_heads = key_rows.shape[1] // HD
    group_size = queries.shape[1] // HD // kv_heads
    score_scale = HD ** -0.5
    hi = lax.Precision.HIGHEST
    starts = jnp.cumsum(equation_lengths) - equation_lengths
    seq_ids = equation_ids(starts, jnp.arange(seq_len, dtype=jnp.int32))
    padded_ids = jnp.concatenate([jnp.full((pad_len,), -1, jnp.int32), seq_ids])
    key_padded = jnp.concatenate([jnp.zeros((pad_len, key_rows.shape[1]), key_rows.dtype), key_rows])
    value_padded = jnp.concatenate([jnp.zeros((pad_len, value_rows.shape[1]), value_rows.dtype), value_rows])
    feat_kv = key_rows.shape[1]

    def one_block(carry, block_index):
        key_acc, value_acc = carry
        first = (block_index * block_len).astype(jnp.int32)
        query_blk = lax.dynamic_slice_in_dim(queries, first, block_len, 0).astype(jnp.float32).reshape(block_len, kv_heads, group_size, HD)
        grad_blk = lax.dynamic_slice_in_dim(cotangent, first, block_len, 0).astype(jnp.float32).reshape(block_len, kv_heads, group_size, HD)
        key_win = lax.dynamic_slice_in_dim(key_padded, first, window, 0).astype(jnp.float32).reshape(window, kv_heads, HD)
        value_win = lax.dynamic_slice_in_dim(value_padded, first, window, 0).astype(jnp.float32).reshape(window, kv_heads, HD)
        query_pos = first + jnp.arange(block_len, dtype=jnp.int32)
        key_pos = first - pad_len + jnp.arange(window, dtype=jnp.int32)
        query_ids = lax.dynamic_slice_in_dim(seq_ids, first, block_len, 0)
        key_ids = lax.dynamic_slice_in_dim(padded_ids, first, window, 0)
        allowed = (key_pos[None, :] >= 0) & (key_pos[None, :] <= query_pos[:, None]) & (key_ids[None, :] == query_ids[:, None])
        scores = jnp.einsum("qhgd,khd->hgqk", query_blk, key_win, precision=hi) * score_scale
        scores = jnp.where(allowed[None, None], scores, -jnp.inf)
        top = jnp.max(scores, axis=-1)
        log_total = top + jnp.log(jnp.sum(jnp.exp(scores - top[..., None]), axis=-1))
        weights = jnp.exp(scores - log_total[..., None])
        weights_low = weights.astype(jnp.bfloat16).astype(jnp.float32)
        attn_blk = jnp.einsum("hgqk,khd->qhgd", weights_low, value_win, precision=hi).astype(jnp.bfloat16)
        delta = jnp.transpose(jnp.sum(grad_blk * attn_blk.astype(jnp.float32), axis=-1), (1, 2, 0))
        weight_grad = jnp.einsum("qhgd,khd->hgqk", grad_blk, value_win, precision=hi)
        score_grad = (weights * (weight_grad - delta[..., None])).astype(jnp.bfloat16).astype(jnp.float32)
        query_part = (jnp.einsum("hgqk,khd->qhgd", score_grad, key_win, precision=hi) * score_scale).astype(jnp.bfloat16)
        key_part = jnp.einsum("hgqk,qhgd->khd", score_grad, query_blk, precision=hi) * score_scale
        value_part = jnp.einsum("hgqk,qhgd->khd", weights_low, grad_blk, precision=hi)
        key_acc = lax.dynamic_update_slice_in_dim(key_acc, lax.dynamic_slice_in_dim(key_acc, first, window, 0) + key_part.reshape(window, feat_kv), first, 0)
        value_acc = lax.dynamic_update_slice_in_dim(value_acc, lax.dynamic_slice_in_dim(value_acc, first, window, 0) + value_part.reshape(window, feat_kv), first, 0)
        return (key_acc, value_acc), (attn_blk.reshape(block_len, -1), query_part.reshape(block_len, -1))

    empty = jnp.zeros((pad_len + seq_len, feat_kv), jnp.float32)
    (key_acc, value_acc), (attn_all, query_all) = lax.scan(one_block, (empty, empty), jnp.arange(block_count, dtype=jnp.int32))
    attention = attn_all.reshape(seq_len, -1)
    query_grad = query_all.reshape(seq_len, -1)
    key_grad = key_acc[pad_len:].astype(jnp.bfloat16)
    value_grad = value_acc[pad_len:].astype(jnp.bfloat16)
    return (attention, query_grad, key_grad, value_grad)
```

```python
import functools

import jax
import jax.numpy as jnp
from jax import lax
from jax.experimental import pallas as pl
from jax.experimental.pallas import tpu as pltpu
from jax.sharding import PartitionSpec as P

HD = 128
REACH = 4
LOG2E = 1.4426950408889634
MASKED = -1e30


def shifted(value, steps):
    count = lax.axis_size("ctx")
    first, last = max(0, -steps), min(count, count - steps)
    return lax.ppermute(value, "ctx", [(i, i + steps) for i in range(first, last)])


def swapped(value):
    return lax.ppermute(value, "ctx", [(i, i ^ 1) for i in range(lax.axis_size("ctx"))])


def attend_kernel(tk, heads, len_ref, ctx_ref, q_ref, g_ref, own_ref, r2_ref, r4_ref, b_ref, a_ref,
                  out_ref, down_ref, d2_ref, d4_ref, db_ref, da_ref,
                  k_scr, v_scr, kt_scr, vt_scr, s_scr, acc_scr, qs_scr):
    rows = q_ref.shape[0]
    head = pl.program_id(0)
    ctx = ctx_ref[0]
    odd = lax.rem(ctx, 2)
    base = ctx * rows
    kbase = base - REACH * rows
    docs = len_ref.shape[0]
    scale = HD ** -0.5

    def start_of(pos, zero):
        def body(d, carry):
            run, best = carry
            return run + len_ref[d], jnp.where(run <= pos, run, best)
        return lax.fori_loop(0, docs, body, (jnp.int32(0), zero))[1]

    slot_b, slot_a = 3 - 2 * odd, 1 + 2 * odd

    @pl.when(head == 0)
    def _():
        pos = base + lax.broadcasted_iota(jnp.int32, (8, rows), 1)
        qs_scr[...] = start_of(pos, jnp.zeros((8, rows), jnp.int32))
        for ref, slot in ((r4_ref, 0), (r2_ref, 2), (own_ref, 4), (b_ref, slot_b), (a_ref, slot_a)):
            at = pl.ds(pl.multiple_of(slot * rows, rows), rows)
            keys, values = ref[:, :HD], ref[:, HD:]
            k_scr[at, :] = keys
            v_scr[at, :] = values
            kt_scr[:, at] = keys.T
            vt_scr[:, at] = values.T
        acc_scr[...] = jnp.zeros_like(acc_scr)

    first = start_of(base, jnp.int32(0))
    lo = jnp.maximum(first - kbase, 0) // tk
    hi = (REACH + 1) * rows // tk
    q, g = q_ref[...], g_ref[...]
    q_t, g_t = q.T, g.T
    starts = qs_scr[0:1, :]
    span = base + lax.broadcasted_iota(jnp.int32, (1, rows), 1) - starts
    key_iota = lax.broadcasted_iota(jnp.int32, (tk, rows), 0)

    def scores(t, top):
        at = pl.multiple_of(t * tk, tk)
        s = jnp.dot(k_scr[pl.ds(at, tk), :], q_t, preferred_element_type=jnp.float32)
        s = s * (scale * LOG2E)
        rel = key_iota + (kbase + at - starts)
        s = jnp.where((rel >= 0) & (rel <= span), s, MASKED)
        s_scr[pl.ds(at, tk), :] = s
        return jnp.maximum(top, jnp.max(s.reshape(tk // 8, 8, rows), axis=0))

    top = lax.fori_loop(lo, hi, scores, jnp.full((8, rows), MASKED, jnp.float32))
    top = jnp.max(top, axis=0, keepdims=True)

    def weigh(t, carry):
        total, acc = carry
        at = pl.multiple_of(t * tk, tk)
        p = jnp.exp2(s_scr[pl.ds(at, tk), :] - top)
        s_scr[pl.ds(at, tk), :] = p
        total = total + jnp.sum(p.reshape(tk // 8, 8, rows), axis=0)
        acc = acc + jnp.dot(vt_scr[:, pl.ds(at, tk)], p.astype(jnp.bfloat16),
                            preferred_element_type=jnp.float32)
        return total, acc

    total, acc = lax.fori_loop(
        lo, hi, weigh, (jnp.zeros((8, rows), jnp.float32), jnp.zeros((HD, rows), jnp.float32)))
    inverse = 1.0 / jnp.sum(total, axis=0, keepdims=True)
    attn_t = (acc * inverse).astype(jnp.bfloat16)
    out_ref[:, :HD] = attn_t.T
    delta = jnp.sum(attn_t.astype(jnp.float32) * g_t.astype(jnp.float32), axis=0, keepdims=True)

    def backward(t, dq):
        at = pl.multiple_of(t * tk, tk)
        p = s_scr[pl.ds(at, tk), :] * inverse
        dp = jnp.dot(v_scr[pl.ds(at, tk), :], g_t, preferred_element_type=jnp.float32)
        ds = (p * (dp - delta)).astype(jnp.bfloat16)
        acc_scr[pl.ds(at, tk), :HD] += jnp.dot(ds, q, preferred_element_type=jnp.float32)
        acc_scr[pl.ds(at, tk), HD:] += jnp.dot(
            p.astype(jnp.bfloat16), g, preferred_element_type=jnp.float32)
        return dq + jnp.dot(kt_scr[:, pl.ds(at, tk)], ds, preferred_element_type=jnp.float32)

    dq = lax.fori_loop(lo, hi, backward, jnp.zeros((HD, rows), jnp.float32))
    out_ref[:, HD:] = (dq * scale).astype(jnp.bfloat16).T

    @pl.when(head == heads - 1)
    def _():
        for ref, slot in ((d4_ref, 0), (d2_ref, 2), (down_ref, 4), (db_ref, slot_b), (da_ref, slot_a)):
            at = pl.ds(pl.multiple_of(slot * rows, rows), rows)
            ref[:, :HD] = (acc_scr[at, :HD] * scale).astype(ref.dtype)
            ref[:, HD:] = acc_scr[at, HD:].astype(ref.dtype)


def attend(lengths, ctx, queries, cotangent, blocks, group, heads):
    rows = queries.shape[0]
    window = (REACH + 1) * rows
    tk = rows
    whole = pl.BlockSpec((rows, 2 * HD), lambda h: (0, 0))
    smem = pl.BlockSpec(memory_space=pltpu.SMEM)
    columns = pl.BlockSpec((rows, HD), lambda h: (0, group * heads + h))
    block = jax.ShapeDtypeStruct((rows, 2 * HD), jnp.bfloat16)
    return pl.pallas_call(
        functools.partial(attend_kernel, tk, heads),
        grid=(heads,),
        in_specs=[smem, smem, columns, columns] + [whole] * 5,
        out_specs=[pl.BlockSpec((rows, 2 * HD), lambda h: (0, h))] + [whole] * 5,
        out_shape=[jax.ShapeDtypeStruct((rows, heads * 2 * HD), jnp.bfloat16),
                   jax.ShapeDtypeStruct((rows, 2 * HD), jnp.float32)] + [block] * 4,
        scratch_shapes=[
            pltpu.VMEM((window, HD), jnp.bfloat16),
            pltpu.VMEM((window, HD), jnp.bfloat16),
            pltpu.VMEM((HD, window), jnp.bfloat16),
            pltpu.VMEM((HD, window), jnp.bfloat16),
            pltpu.VMEM((window, rows), jnp.float32),
            pltpu.VMEM((window, 2 * HD), jnp.float32),
            pltpu.VMEM((8, rows), jnp.int32),
        ],
        compiler_params=pltpu.CompilerParams(vmem_limit_bytes=40 * 1024 * 1024),
        cost_estimate=pl.CostEstimate(
            flops=12 * heads * rows * window * HD, bytes_accessed=8 * 1024 * 1024,
            transcendentals=heads * rows * window),
        name="attend",
    )(lengths, ctx, queries, cotangent, *blocks)


def local(queries, key_rows, value_rows, cotangent, lengths):
    rows = queries.shape[0]
    groups = key_rows.shape[1] // HD
    heads = queries.shape[1] // HD // groups
    shares = lax.axis_size("head")
    ctx = lax.axis_index("ctx")
    odd = lax.rem(ctx, 2) == 1
    ctx_in = ctx.astype(jnp.int32).reshape(1)

    def exchanged(value):
        return lax.all_to_all(value.reshape(shares, rows // shares, -1), "head",
                              split_axis=0, concat_axis=0, tiled=True)

    gathered = []
    for group in range(groups):
        cols = slice(group * HD, (group + 1) * HD)
        own = jnp.concatenate([key_rows[:, cols], value_rows[:, cols]], axis=1)
        r2 = shifted(own, 2)
        r4 = shifted(r2, 2)
        b = swapped(r2)
        a = swapped(jnp.where(odd, r4, own))
        gathered.append((own, r2, r4, b, a))

    outs, grads = [], []
    for group in range(groups):
        out, down, d2, d4, db, da = attend(
            lengths, ctx_in, queries, cotangent, gathered[group], group, heads)
        outs.append(exchanged(out))
        back_a = swapped(da)
        back_b = swapped(db)
        far = jnp.where(odd, d4 + back_a, d4)
        back_far = shifted(far, -2)
        mid = (d2.astype(jnp.float32) + back_b.astype(jnp.float32)
               + back_far.astype(jnp.float32)).astype(jnp.bfloat16)
        back_mid = shifted(mid, -2)
        total = down + back_mid.astype(jnp.float32) + jnp.where(odd, 0.0, back_a.astype(jnp.float32))
        grads.append(exchanged(total.astype(jnp.bfloat16)))

    part = rows // shares
    out = jnp.stack([o.reshape(shares, part, heads, 2, HD) for o in outs])
    out = jnp.transpose(out, (4, 2, 1, 0, 3, 5)).reshape(2, part, -1)
    grad = jnp.stack([o.reshape(shares, part, 2, HD) for o in grads])
    grad = jnp.transpose(grad, (3, 2, 1, 0, 4)).reshape(2, part, -1)
    return out[0], out[1], grad[0], grad[1]


def solution(mesh):
    return jax.shard_map(
        local,
        mesh=mesh,
        in_specs=(P("ctx", "head"), P("ctx", "head"), P("ctx", "head"), P("ctx", "head"), P()),
        out_specs=(P(("ctx", "head"), None),) * 4,
        check_vma=False,
    )
```

```python
import functools

import jax
import jax.numpy as jnp
from jax import lax
from jax.experimental import pallas as pl
from jax.experimental.pallas import tpu as pltpu
from jax.sharding import PartitionSpec as P

HD = 128
REACH = 4
LOG2E = 1.4426950408889634
MASKED = -1e30
VMEM_LIMIT = 40


def shifted(value, steps):
    count = lax.axis_size("ctx")
    first, last = max(0, -steps), min(count, count - steps)
    return lax.ppermute(value, "ctx", [(i, i + steps) for i in range(first, last)])


def swapped(value):
    return lax.ppermute(value, "ctx", [(i, i ^ 1) for i in range(lax.axis_size("ctx"))])


def over_rows(a, b):
    return lax.dot_general(a, b, (((0,), (0,)), ((), ())), preferred_element_type=jnp.float32)


def attend_kernel(tq, tk, heads, len_ref, ctx_ref, q_ref, g_ref, own_ref, r2_ref, r4_ref, b_ref, a_ref,
                  out_ref, down_ref, d2_ref, d4_ref, db_ref, da_ref,
                  k_scr, v_scr, p_scr, acc_scr, top_scr, s_scr):
    rows = own_ref.shape[0]
    width = heads * tq
    step_q = pl.program_id(0)
    ctx = ctx_ref[0]
    odd = lax.rem(ctx, 2)
    base = ctx * rows
    kbase = base - REACH * rows
    docs = len_ref.shape[0]
    scale = HD ** -0.5
    bf16 = jnp.bfloat16

    def start_of(pos, zero):
        def body(d, carry):
            run, best = carry
            return run + len_ref[d], jnp.where(run <= pos, run, best)
        return lax.fori_loop(0, docs, body, (jnp.int32(0), zero))[1]

    slot_b, slot_a = 3 - 2 * odd, 1 + 2 * odd

    @pl.when(step_q == 0)
    def _():
        for ref, slot in ((r4_ref, 0), (r2_ref, 2), (own_ref, 4), (b_ref, slot_b), (a_ref, slot_a)):
            at = pl.ds(pl.multiple_of(tk + slot * rows, rows), rows)
            k_scr[at, :] = ref[:, :HD]
            v_scr[at, :] = ref[:, HD:]
        k_scr[:tk, :] = jnp.zeros((tk, HD), bf16)
        v_scr[:tk, :] = jnp.zeros((tk, HD), bf16)
        acc_scr[...] = jnp.zeros_like(acc_scr)

    q0 = step_q * tq
    end = REACH * rows + q0 + tq
    first = jnp.maximum(start_of(base + q0, jnp.int32(0)) - kbase, 0)
    last = jnp.maximum(start_of(base + q0 + tq - 1, jnp.int32(0)) - kbase, 0)
    tiles = (end - first + tk - 1) // tk
    whole = jnp.clip((end - last) // tk, 1, tiles)

    q = jnp.concatenate([q_ref[:, h * HD:(h + 1) * HD] for h in range(heads)], axis=0)
    g = jnp.concatenate([g_ref[:, h * HD:(h + 1) * HD] for h in range(heads)], axis=0)
    q_t, g_t = q.T, g.T
    q_pos = base + q0 + lax.rem(lax.broadcasted_iota(jnp.int32, (8, width), 1), tq)
    starts = start_of(q_pos, jnp.zeros((8, width), jnp.int32))[0:1, :]
    span = q_pos[0:1, :] - starts
    key_iota = lax.broadcasted_iota(jnp.int32, (tk, width), 0)

    def tile(t):
        return pl.ds(pl.multiple_of(tk + end - (t + 1) * tk, HD), tk)

    def scores(t, masked):
        s = jnp.dot(k_scr[tile(t), :], q_t, preferred_element_type=jnp.float32) * (scale * LOG2E)
        if masked:
            rel = key_iota + (kbase + end - (t + 1) * tk - starts)
            s = jnp.where((rel >= 0) & (rel <= span), s, MASKED)
        return s

    def top_of(top, s):
        return jnp.maximum(top, jnp.max(s, axis=0, keepdims=True))

    def weigh(t, before, top, total, acc, s):
        p = jnp.exp2(s - top)
        p_scr[tile(t), :] = p
        top_scr[t] = jnp.broadcast_to(top, (8, width))
        fade = jnp.exp2(before - top)
        total = total * fade + jnp.sum(p.reshape(tk // 8, 8, width), axis=0)
        return total, acc * fade + over_rows(v_scr[tile(t), :], p.astype(bf16))

    def forward(masked, t, carry):
        before, top, total, acc = carry
        s = s_scr[...]
        following = scores(t + 1, masked)
        new_top = top_of(top, following)
        total, acc = weigh(t, before, top, total, acc, s)
        s_scr[...] = following
        return top, new_top, total, acc

    s = scores(0, True)
    top = top_of(jnp.full((1, width), MASKED, jnp.float32), s)
    s_scr[...] = s
    carry = (top, top, jnp.zeros((8, width), jnp.float32), jnp.zeros((HD, width), jnp.float32))
    carry = lax.fori_loop(0, whole - 1, functools.partial(forward, False), carry)
    before, top, total, acc = lax.fori_loop(whole - 1, tiles - 1, functools.partial(forward, True), carry)
    total, acc = weigh(tiles - 1, before, top, total, acc, s_scr[...])
    inverse = 1.0 / jnp.sum(total, axis=0, keepdims=True)
    attn_t = (acc * inverse).astype(bf16)
    delta = jnp.sum(attn_t.astype(jnp.float32) * g_t.astype(jnp.float32), axis=0, keepdims=True)

    def backward(t, dq):
        p = p_scr[tile(t), :] * (jnp.exp2(top_scr[t][0:1, :] - top) * inverse)
        dp = jnp.dot(v_scr[tile(t), :], g_t, preferred_element_type=jnp.float32)
        ds = (p * (dp - delta)).astype(bf16)
        acc_scr[tile(t), HD:] += jnp.dot(p.astype(bf16), g, preferred_element_type=jnp.float32)
        acc_scr[tile(t), :HD] += jnp.dot(ds, q, preferred_element_type=jnp.float32)
        return dq + over_rows(k_scr[tile(t), :], ds)

    dq_t = lax.fori_loop(0, tiles, backward, jnp.zeros((HD, width), jnp.float32))
    attn, dq = attn_t.T, (dq_t * scale).astype(bf16).T
    for h in range(heads):
        out_ref[:, 2 * h * HD:(2 * h + 1) * HD] = attn[h * tq:(h + 1) * tq, :]
        out_ref[:, (2 * h + 1) * HD:(2 * h + 2) * HD] = dq[h * tq:(h + 1) * tq, :]

    @pl.when(step_q == pl.num_programs(0) - 1)
    def _():
        for ref, slot in ((d4_ref, 0), (d2_ref, 2), (down_ref, 4), (db_ref, slot_b), (da_ref, slot_a)):
            at = pl.ds(pl.multiple_of(tk + slot * rows, rows), rows)
            ref[:, :HD] = (acc_scr[at, :HD] * scale).astype(ref.dtype)
            ref[:, HD:] = acc_scr[at, HD:].astype(ref.dtype)


def attend(lengths, ctx, queries, cotangent, blocks, group, heads):
    rows = queries.shape[0]
    tq, tk = min(256, rows), rows
    window = (REACH + 1) * rows
    whole = pl.BlockSpec((rows, 2 * HD), lambda t: (0, 0))
    smem = pl.BlockSpec(memory_space=pltpu.SMEM)
    columns = pl.BlockSpec((tq, heads * HD), lambda t: (t, group))
    block = jax.ShapeDtypeStruct((rows, 2 * HD), jnp.bfloat16)
    return pl.pallas_call(
        functools.partial(attend_kernel, tq, tk, heads),
        grid=(rows // tq,),
        in_specs=[smem, smem, columns, columns] + [whole] * 5,
        out_specs=[pl.BlockSpec((tq, heads * 2 * HD), lambda t: (t, 0))] + [whole] * 5,
        out_shape=[jax.ShapeDtypeStruct((rows, heads * 2 * HD), jnp.bfloat16),
                   jax.ShapeDtypeStruct((rows, 2 * HD), jnp.float32)] + [block] * 4,
        scratch_shapes=[
            pltpu.VMEM((window + tk, HD), jnp.bfloat16),
            pltpu.VMEM((window + tk, HD), jnp.bfloat16),
            pltpu.VMEM((window + tk, heads * tq), jnp.float32),
            pltpu.VMEM((window + tk, 2 * HD), jnp.float32),
            pltpu.VMEM((window // tk + 1, 8, heads * tq), jnp.float32),
            pltpu.VMEM((tk, heads * tq), jnp.float32),
        ],
        compiler_params=pltpu.CompilerParams(vmem_limit_bytes=VMEM_LIMIT * 1024 * 1024),
        cost_estimate=pl.CostEstimate(
            flops=12 * heads * rows * window * HD, bytes_accessed=8 * 1024 * 1024,
            transcendentals=heads * rows * window),
        name="attend",
    )(lengths, ctx, queries, cotangent, *blocks)


def unpack_kernel(groups, heads, *refs):
    first_ref, second_ref = refs[groups:]
    shares = refs[0].shape[0]
    for share in range(shares):
        for group in range(groups):
            for head in range(heads):
                column = ((share * groups + group) * heads + head) * HD
                source = 2 * head * HD
                first_ref[:, column:column + HD] = refs[group][share, :, source:source + HD]
                second_ref[:, column:column + HD] = refs[group][share, :, source + HD:source + 2 * HD]


def unpacked(received, heads):
    groups = len(received)
    shares, part, _ = received[0].shape
    out = jax.ShapeDtypeStruct((part, shares * groups * heads * HD), jnp.bfloat16)
    return pl.pallas_call(
        functools.partial(unpack_kernel, groups, heads),
        out_shape=[out] * 2,
        name="unpack",
    )(*received)


def local(queries, key_rows, value_rows, cotangent, lengths):
    rows = queries.shape[0]
    groups = key_rows.shape[1] // HD
    heads = queries.shape[1] // HD // groups
    shares = lax.axis_size("head")
    ctx = lax.axis_index("ctx")
    odd = lax.rem(ctx, 2) == 1
    ctx_in = ctx.astype(jnp.int32).reshape(1)

    def exchanged(value):
        return lax.all_to_all(value.reshape(shares, rows // shares, -1), "head",
                              split_axis=0, concat_axis=0, tiled=True)

    gathered = []
    for group in range(groups):
        cols = slice(group * HD, (group + 1) * HD)
        own = jnp.concatenate([key_rows[:, cols], value_rows[:, cols]], axis=1)
        r2 = shifted(own, 2)
        r4 = shifted(r2, 2)
        b = swapped(r2)
        a = shifted(jnp.where(odd, r2, own), 1)
        gathered.append((own, r2, r4, b, a))

    outs, totals = [], []
    for group in range(groups):
        produced = attend(lengths, ctx_in, queries, cotangent, gathered[group], group, heads)
        if outs:
            outs[-1], produced = lax.optimization_barrier((outs[-1], produced))
        out, down, d2, d4, db, da = produced
        back_4 = shifted(d4, -2)
        back_a = shifted(da, -1)
        back_b = swapped(db)
        outs.append(exchanged(out))
        wide_a = back_a.astype(jnp.float32)
        mid = (d2.astype(jnp.float32) + back_b.astype(jnp.float32)
               + back_4.astype(jnp.float32) + jnp.where(odd, wide_a, 0.0))
        back_2 = shifted(mid.astype(jnp.bfloat16), -2)
        totals.append((down, back_2, wide_a))

    attention, query_grad = unpacked(outs, heads)
    attention, query_grad, totals = lax.optimization_barrier((attention, query_grad, totals))
    grads = [(down + back_2.astype(jnp.float32) + jnp.where(odd, 0.0, wide_a)).astype(jnp.bfloat16)
             for down, back_2, wide_a in totals]
    key_grad, value_grad = unpacked([exchanged(jnp.concatenate(grads, axis=1))], groups)
    return attention, query_grad, key_grad, value_grad


def solution(mesh):
    return jax.shard_map(
        local,
        mesh=mesh,
        in_specs=(P("ctx", "head"), P("ctx", "head"), P("ctx", "head"), P("ctx", "head"), P()),
        out_specs=(P(("ctx", "head"), None),) * 4,
        check_vma=False,
    )
```

```python
import functools

import jax
import jax.numpy as jnp
from jax import lax
from jax.experimental import pallas as pl
from jax.experimental.pallas import tpu as pltpu
from jax.sharding import PartitionSpec as P

HD = 128
REACH = 4
LOG2E = 1.4426950408889634
MASKED = -1e30
VMEM_LIMIT = 40


def shifted(value, steps):
    count = lax.axis_size("ctx")
    first, last = max(0, -steps), min(count, count - steps)
    return lax.ppermute(value, "ctx", [(i, i + steps) for i in range(first, last)])


def swapped(value):
    return lax.ppermute(value, "ctx", [(i, i ^ 1) for i in range(lax.axis_size("ctx"))])


def over_rows(a, b):
    return lax.dot_general(a, b, (((0,), (0,)), ((), ())), preferred_element_type=jnp.float32)


def attend_kernel(tq, tk, heads, len_ref, ctx_ref, q_ref, g_ref, own_ref, r2_ref, r4_ref, b_ref, a_ref,
                  out_ref, down_ref, d2_ref, d4_ref, db_ref, da_ref,
                  k_scr, v_scr, p_scr, acc_scr, top_scr, s_scr):
    rows = own_ref.shape[0]
    width = heads * tq
    step_q = pl.program_id(0)
    ctx = ctx_ref[0]
    odd = lax.rem(ctx, 2)
    base = ctx * rows
    kbase = base - REACH * rows
    docs = len_ref.shape[0]
    scale = HD ** -0.5
    bf16 = jnp.bfloat16

    def start_of(pos, zero):
        def body(d, carry):
            run, best = carry
            return run + len_ref[d], jnp.where(run <= pos, run, best)
        return lax.fori_loop(0, docs, body, (jnp.int32(0), zero))[1]

    slot_b, slot_a = 3 - 2 * odd, 1 + 2 * odd

    @pl.when(step_q == 0)
    def _():
        for ref, slot in ((r4_ref, 0), (r2_ref, 2), (own_ref, 4), (b_ref, slot_b), (a_ref, slot_a)):
            at = pl.ds(pl.multiple_of(tk + slot * rows, rows), rows)
            k_scr[at, :] = ref[:, :HD]
            v_scr[at, :] = ref[:, HD:]
        k_scr[:tk, :] = jnp.zeros((tk, HD), bf16)
        v_scr[:tk, :] = jnp.zeros((tk, HD), bf16)
        acc_scr[...] = jnp.zeros_like(acc_scr)

    q0 = step_q * tq
    end = REACH * rows + q0 + tq
    first = jnp.maximum(start_of(base + q0, jnp.int32(0)) - kbase, 0)
    last = jnp.maximum(start_of(base + q0 + tq - 1, jnp.int32(0)) - kbase, 0)
    tiles = (end - first + tk - 1) // tk
    whole = jnp.clip((end - last) // tk, 1, tiles)

    q = jnp.concatenate([q_ref[:, h * HD:(h + 1) * HD] for h in range(heads)], axis=0)
    g = jnp.concatenate([g_ref[:, h * HD:(h + 1) * HD] for h in range(heads)], axis=0)
    q_t, g_t = q.T, g.T
    q_pos = base + q0 + lax.rem(lax.broadcasted_iota(jnp.int32, (8, width), 1), tq)
    starts = start_of(q_pos, jnp.zeros((8, width), jnp.int32))[0:1, :]
    span = q_pos[0:1, :] - starts
    key_iota = lax.broadcasted_iota(jnp.int32, (tk, width), 0)

    def tile(t):
        return pl.ds(pl.multiple_of(tk + end - (t + 1) * tk, HD), tk)

    def scores(t, masked):
        s = jnp.dot(k_scr[tile(t), :], q_t, preferred_element_type=jnp.float32) * (scale * LOG2E)
        if masked:
            before = starts - (kbase + end - (t + 1) * tk)
            inside = key_iota >= before
            if masked == "both":
                inside &= key_iota <= before + span
            s = jnp.where(inside, s, MASKED)
        return s

    def top_of(top, s):
        return jnp.maximum(top, jnp.max(s, axis=0, keepdims=True))

    def weigh(t, before, top, total, acc, s):
        p = jnp.exp2(s - top)
        p_scr[tile(t), :] = p
        top_scr[t] = jnp.broadcast_to(top, (8, width))
        fade = jnp.exp2(before - top)
        total = total * fade + jnp.sum(p.reshape(tk // 8, 8, width), axis=0)
        return total, acc * fade + over_rows(v_scr[tile(t), :], p.astype(bf16))

    def forward(masked, t, carry):
        before, top, total, acc = carry
        s = s_scr[...]
        following = scores(t + 1, masked)
        new_top = top_of(top, following)
        total, acc = weigh(t, before, top, total, acc, s)
        s_scr[...] = following
        return top, new_top, total, acc

    s = scores(0, "both")
    top = top_of(jnp.full((1, width), MASKED, jnp.float32), s)
    s_scr[...] = s
    carry = (top, top, jnp.zeros((8, width), jnp.float32), jnp.zeros((HD, width), jnp.float32))
    carry = lax.fori_loop(0, whole - 1, functools.partial(forward, False), carry)
    before, top, total, acc = lax.fori_loop(whole - 1, tiles - 1, functools.partial(forward, True), carry)
    total, acc = weigh(tiles - 1, before, top, total, acc, s_scr[...])
    inverse = 1.0 / jnp.sum(total, axis=0, keepdims=True)
    attn_t = (acc * inverse).astype(bf16)
    delta = jnp.sum(attn_t.astype(jnp.float32) * g_t.astype(jnp.float32), axis=0, keepdims=True)

    def backward(t, dq):
        p = p_scr[tile(t), :] * (jnp.exp2(top_scr[t][0:1, :] - top) * inverse)
        dp = jnp.dot(v_scr[tile(t), :], g_t, preferred_element_type=jnp.float32)
        ds = (p * (dp - delta)).astype(bf16)
        acc_scr[tile(t), HD:] += jnp.dot(p.astype(bf16), g, preferred_element_type=jnp.float32)
        acc_scr[tile(t), :HD] += jnp.dot(ds, q, preferred_element_type=jnp.float32)
        return dq + over_rows(k_scr[tile(t), :], ds)

    dq_t = lax.fori_loop(0, tiles, backward, jnp.zeros((HD, width), jnp.float32))
    attn, dq = attn_t.T, (dq_t * scale).astype(bf16).T
    for h in range(heads):
        out_ref[:, 2 * h * HD:(2 * h + 1) * HD] = attn[h * tq:(h + 1) * tq, :]
        out_ref[:, (2 * h + 1) * HD:(2 * h + 2) * HD] = dq[h * tq:(h + 1) * tq, :]

    @pl.when(step_q == pl.num_programs(0) - 1)
    def _():
        for ref, slot in ((d4_ref, 0), (d2_ref, 2), (down_ref, 4), (db_ref, slot_b), (da_ref, slot_a)):
            at = pl.ds(pl.multiple_of(tk + slot * rows, rows), rows)
            ref[:, :HD] = (acc_scr[at, :HD] * scale).astype(ref.dtype)
            ref[:, HD:] = acc_scr[at, HD:].astype(ref.dtype)


def attend(lengths, ctx, queries, cotangent, blocks, group, heads):
    rows = queries.shape[0]
    tq, tk = min(256, rows), rows
    window = (REACH + 1) * rows
    whole = pl.BlockSpec((rows, 2 * HD), lambda t: (0, 0))
    smem = pl.BlockSpec(memory_space=pltpu.SMEM)
    columns = pl.BlockSpec((tq, heads * HD), lambda t: (t, group))
    block = jax.ShapeDtypeStruct((rows, 2 * HD), jnp.bfloat16)
    queries, cotangent = (pltpu.with_memory_space_constraint(x, pltpu.HBM) for x in (queries, cotangent))
    return pl.pallas_call(
        functools.partial(attend_kernel, tq, tk, heads),
        grid=(rows // tq,),
        in_specs=[smem, smem, columns, columns] + [whole] * 5,
        out_specs=[pl.BlockSpec((tq, heads * 2 * HD), lambda t: (t, 0))] + [whole] * 5,
        out_shape=[jax.ShapeDtypeStruct((rows, heads * 2 * HD), jnp.bfloat16),
                   jax.ShapeDtypeStruct((rows, 2 * HD), jnp.float32)] + [block] * 4,
        scratch_shapes=[
            pltpu.VMEM((window + tk, HD), jnp.bfloat16),
            pltpu.VMEM((window + tk, HD), jnp.bfloat16),
            pltpu.VMEM((window + tk, heads * tq), jnp.float32),
            pltpu.VMEM((window + tk, 2 * HD), jnp.float32),
            pltpu.VMEM((window // tk + 1, 8, heads * tq), jnp.float32),
            pltpu.VMEM((tk, heads * tq), jnp.float32),
        ],
        compiler_params=pltpu.CompilerParams(vmem_limit_bytes=VMEM_LIMIT * 1024 * 1024),
        cost_estimate=pl.CostEstimate(
            flops=12 * heads * rows * window * HD, bytes_accessed=8 * 1024 * 1024,
            transcendentals=heads * rows * window),
        name="attend",
    )(lengths, ctx, queries, cotangent, *blocks)


def unpack_kernel(groups, heads, *refs):
    first_ref, second_ref = refs[groups:]
    shares = refs[0].shape[0]
    for share in range(shares):
        for group in range(groups):
            for head in range(heads):
                column = ((share * groups + group) * heads + head) * HD
                source = 2 * head * HD
                first_ref[:, column:column + HD] = refs[group][share, :, source:source + HD]
                second_ref[:, column:column + HD] = refs[group][share, :, source + HD:source + 2 * HD]


def unpacked(received, heads):
    groups = len(received)
    shares, part, _ = received[0].shape
    out = jax.ShapeDtypeStruct((part, shares * groups * heads * HD), jnp.bfloat16)
    return pl.pallas_call(
        functools.partial(unpack_kernel, groups, heads),
        out_shape=[out] * 2,
        name="unpack",
    )(*received)


def local(queries, key_rows, value_rows, cotangent, lengths):
    rows = queries.shape[0]
    groups = key_rows.shape[1] // HD
    heads = queries.shape[1] // HD // groups
    shares = lax.axis_size("head")
    ctx = lax.axis_index("ctx")
    odd = lax.rem(ctx, 2) == 1
    ctx_in = ctx.astype(jnp.int32).reshape(1)

    def exchanged(value):
        return lax.all_to_all(value.reshape(shares, rows // shares, -1), "head",
                              split_axis=0, concat_axis=0, tiled=True)

    def hop_sum(back, parts):
        back_4, back_a, back_b = (x.astype(jnp.float32) for x in back)
        own, d2 = parts
        mid = d2.astype(jnp.float32) + back_b + back_4 + jnp.where(odd, back_a, 0.0)
        return own + jnp.where(odd, 0.0, back_a), shifted(mid.astype(jnp.bfloat16), -2)

    gathered = []
    for group in range(groups):
        cols = slice(group * HD, (group + 1) * HD)
        own = jnp.concatenate([key_rows[:, cols], value_rows[:, cols]], axis=1)
        r2 = shifted(own, 2)
        r4 = shifted(r2, 2)
        b = swapped(r2)
        a = shifted(jnp.where(odd, r2, own), 1)
        gathered.append((own, r2, r4, b, a))

    tie = lax.optimization_barrier
    received, sums, moving = [], [], None
    for group in range(groups):
        produced = attend(lengths, ctx_in, queries, cotangent, gathered[group], group, heads)
        if group:
            (out, back), produced = tie(((exchanged(moving[0]), moving[1]), produced))
            received.append(out)
            sums.append(hop_sum(back, moving[2]))
        out, down, d2, d4, db, da = produced
        back = (shifted(d4, -2), shifted(da, -1), swapped(db))
        moving = (out, back, (down, d2))
    out, back, parts = moving
    out, swapped_back = tie((out, back[2]))
    received.append(exchanged(out))
    sums.append(hop_sum(back[:2] + (swapped_back,), parts))

    grads = jnp.concatenate([own + back_2.astype(jnp.float32) for own, back_2 in sums], axis=1)
    grads = exchanged(grads.astype(jnp.bfloat16))
    attention, query_grad = unpacked(received, heads)
    attention, query_grad, grads = tie((attention, query_grad, grads))
    key_grad, value_grad = unpacked([grads], groups)
    return attention, query_grad, key_grad, value_grad


def solution(mesh):
    return jax.shard_map(
        local,
        mesh=mesh,
        in_specs=(P("ctx", "head"), P("ctx", "head"), P("ctx", "head"), P("ctx", "head"), P()),
        out_specs=(P(("ctx", "head"), None),) * 4,
        check_vma=False,
    )
```

```python
import functools

import jax
import jax.numpy as jnp
from jax import lax
from jax.experimental import pallas as pl
from jax.experimental.pallas import tpu as pltpu
from jax.sharding import PartitionSpec as P

HD = 128
REACH = 4
LOG2E = 1.4426950408889634
MASKED = -1e30
VMEM_LIMIT = 40


def shifted(value, steps):
    count = lax.axis_size("ctx")
    first, last = max(0, -steps), min(count, count - steps)
    return lax.ppermute(value, "ctx", [(i, i + steps) for i in range(first, last)])


def swapped(value):
    return lax.ppermute(value, "ctx", [(i, i ^ 1) for i in range(lax.axis_size("ctx"))])


def over_rows(a, b):
    return lax.dot_general(a, b, (((0,), (0,)), ((), ())), preferred_element_type=jnp.float32)


def attend_kernel(tq, tk, heads, len_ref, ctx_ref, q_ref, g_ref, own_ref, near_ref, r2_ref, r4_ref, b_ref, a_ref,
                  out_ref, down_ref, d2_ref, d4_ref, db_ref, da_ref,
                  k_scr, v_scr, p_scr, acc_scr, top_scr, s_scr):
    rows = own_ref.shape[0]
    width = heads * tq
    step_q = pl.program_id(0)
    ctx = ctx_ref[0]
    odd = lax.rem(ctx, 2)
    base = ctx * rows
    kbase = base - REACH * rows
    docs = len_ref.shape[0]
    scale = HD ** -0.5
    bf16 = jnp.bfloat16

    def start_of(pos, zero):
        def body(d, carry):
            run, best = carry
            return run + len_ref[d], jnp.where(run <= pos, run, best)
        return lax.fori_loop(0, docs, body, (jnp.int32(0), zero))[1]

    slot_b, slot_a = 3 - 2 * odd, 1 + 2 * odd

    @pl.when(step_q == 0)
    def _():
        def place(ref, slot):
            at = pl.ds(pl.multiple_of(tk + slot * rows, rows), rows)
            k_scr[at, :] = ref[:, :HD]
            v_scr[at, :] = ref[:, HD:]

        for ref, slot in ((r4_ref, 0), (r2_ref, 2), (own_ref, 4), (b_ref, slot_b)):
            place(ref, slot)
        pl.when(odd == 1)(lambda: place(near_ref, 3))
        pl.when(odd == 0)(lambda: place(a_ref, 1))
        k_scr[:tk, :] = jnp.zeros((tk, HD), bf16)
        v_scr[:tk, :] = jnp.zeros((tk, HD), bf16)
        acc_scr[...] = jnp.zeros_like(acc_scr)

    q0 = step_q * tq
    end = REACH * rows + q0 + tq
    first = jnp.maximum(start_of(base + q0, jnp.int32(0)) - kbase, 0)
    last = jnp.maximum(start_of(base + q0 + tq - 1, jnp.int32(0)) - kbase, 0)
    tiles = (end - first + tk - 1) // tk
    whole = jnp.clip((end - last) // tk, 1, tiles)

    q = jnp.concatenate([q_ref[:, h * HD:(h + 1) * HD] for h in range(heads)], axis=0)
    g = jnp.concatenate([g_ref[:, h * HD:(h + 1) * HD] for h in range(heads)], axis=0)
    q_t, g_t = q.T, g.T
    q_pos = base + q0 + lax.rem(lax.broadcasted_iota(jnp.int32, (8, width), 1), tq)
    starts = start_of(q_pos, jnp.zeros((8, width), jnp.int32))[0:1, :]
    span = q_pos[0:1, :] - starts
    key_iota = lax.broadcasted_iota(jnp.int32, (tk, width), 0)

    def tile(t):
        return pl.ds(pl.multiple_of(tk + end - (t + 1) * tk, HD), tk)

    def scores(t, masked):
        s = jnp.dot(k_scr[tile(t), :], q_t, preferred_element_type=jnp.float32) * (scale * LOG2E)
        if masked:
            before = starts - (kbase + end - (t + 1) * tk)
            inside = key_iota >= before
            if masked == "both":
                inside &= key_iota <= before + span
            s = jnp.where(inside, s, MASKED)
        return s

    def top_of(top, s):
        return jnp.maximum(top, jnp.max(s, axis=0, keepdims=True))

    def weigh(t, before, top, total, acc, s):
        p = jnp.exp2(s - top)
        p_scr[tile(t), :] = p
        top_scr[t] = jnp.broadcast_to(top, (8, width))
        fade = jnp.exp2(before - top)
        total = total * fade + jnp.sum(p.reshape(tk // 8, 8, width), axis=0)
        return total, acc * fade + over_rows(v_scr[tile(t), :], p.astype(bf16))

    def forward(masked, t, carry):
        before, top, total, acc = carry
        s = s_scr[...]
        following = scores(t + 1, masked)
        new_top = top_of(top, following)
        total, acc = weigh(t, before, top, total, acc, s)
        s_scr[...] = following
        return top, new_top, total, acc

    s = scores(0, "both")
    top = top_of(jnp.full((1, width), MASKED, jnp.float32), s)
    s_scr[...] = s
    carry = (top, top, jnp.zeros((8, width), jnp.float32), jnp.zeros((HD, width), jnp.float32))
    carry = lax.fori_loop(0, whole - 1, functools.partial(forward, False), carry)
    before, top, total, acc = lax.fori_loop(whole - 1, tiles - 1, functools.partial(forward, True), carry)
    total, acc = weigh(tiles - 1, before, top, total, acc, s_scr[...])
    inverse = 1.0 / jnp.sum(total, axis=0, keepdims=True)
    attn_t = (acc * inverse).astype(bf16)
    delta = jnp.sum(attn_t.astype(jnp.float32) * g_t.astype(jnp.float32), axis=0, keepdims=True)

    def backward(t, dq):
        p = p_scr[tile(t), :] * (jnp.exp2(top_scr[t][0:1, :] - top) * inverse)
        dp = jnp.dot(v_scr[tile(t), :], g_t, preferred_element_type=jnp.float32)
        ds = (p * (dp - delta)).astype(bf16)
        acc_scr[tile(t), HD:] += jnp.dot(p.astype(bf16), g, preferred_element_type=jnp.float32)
        acc_scr[tile(t), :HD] += jnp.dot(ds, q, preferred_element_type=jnp.float32)
        return dq + over_rows(k_scr[tile(t), :], ds)

    dq_t = lax.fori_loop(0, tiles, backward, jnp.zeros((HD, width), jnp.float32))
    attn, dq = attn_t.T, (dq_t * scale).astype(bf16).T
    for h in range(heads):
        out_ref[:, 2 * h * HD:(2 * h + 1) * HD] = attn[h * tq:(h + 1) * tq, :]
        out_ref[:, (2 * h + 1) * HD:(2 * h + 2) * HD] = dq[h * tq:(h + 1) * tq, :]

    @pl.when(step_q == pl.num_programs(0) - 1)
    def _():
        for ref, slot in ((d4_ref, 0), (d2_ref, 2), (down_ref, 4), (db_ref, slot_b), (da_ref, slot_a)):
            at = pl.ds(pl.multiple_of(tk + slot * rows, rows), rows)
            ref[:, :HD] = (acc_scr[at, :HD] * scale).astype(ref.dtype)
            ref[:, HD:] = acc_scr[at, HD:].astype(ref.dtype)


def attend(lengths, ctx, queries, cotangent, blocks, group, heads):
    rows = queries.shape[0]
    tq, tk = min(256, rows), rows
    window = (REACH + 1) * rows
    whole = pl.BlockSpec((rows, 2 * HD), lambda t: (0, 0))
    smem = pl.BlockSpec(memory_space=pltpu.SMEM)
    columns = pl.BlockSpec((tq, heads * HD), lambda t: (t, group))
    block = jax.ShapeDtypeStruct((rows, 2 * HD), jnp.bfloat16)
    queries, cotangent, *blocks = (
        pltpu.with_memory_space_constraint(x, pltpu.HBM) for x in (queries, cotangent, *blocks))
    return pl.pallas_call(
        functools.partial(attend_kernel, tq, tk, heads),
        grid=(rows // tq,),
        in_specs=[smem, smem, columns, columns] + [whole] * 6,
        out_specs=[pl.BlockSpec((tq, heads * 2 * HD), lambda t: (t, 0))] + [whole] * 5,
        out_shape=[jax.ShapeDtypeStruct((rows, heads * 2 * HD), jnp.bfloat16),
                   jax.ShapeDtypeStruct((rows, 2 * HD), jnp.float32)] + [block] * 4,
        scratch_shapes=[
            pltpu.VMEM((window + tk, HD), jnp.bfloat16),
            pltpu.VMEM((window + tk, HD), jnp.bfloat16),
            pltpu.VMEM((window + tk, heads * tq), jnp.float32),
            pltpu.VMEM((window + tk, 2 * HD), jnp.float32),
            pltpu.VMEM((window // tk + 1, 8, heads * tq), jnp.float32),
            pltpu.VMEM((tk, heads * tq), jnp.float32),
        ],
        compiler_params=pltpu.CompilerParams(vmem_limit_bytes=VMEM_LIMIT * 1024 * 1024),
        cost_estimate=pl.CostEstimate(
            flops=12 * heads * rows * window * HD, bytes_accessed=8 * 1024 * 1024,
            transcendentals=heads * rows * window),
        name="attend",
    )(lengths, ctx, queries, cotangent, *blocks)


def unpack_kernel(groups, heads, *refs):
    first_ref, second_ref = refs[groups:]
    shares = refs[0].shape[0]
    for share in range(shares):
        for group in range(groups):
            for head in range(heads):
                column = ((share * groups + group) * heads + head) * HD
                source = 2 * head * HD
                first_ref[:, column:column + HD] = refs[group][share, :, source:source + HD]
                second_ref[:, column:column + HD] = refs[group][share, :, source + HD:source + 2 * HD]


def unpacked(received, heads):
    groups = len(received)
    shares, part, _ = received[0].shape
    out = jax.ShapeDtypeStruct((part, shares * groups * heads * HD), jnp.bfloat16)
    return pl.pallas_call(
        functools.partial(unpack_kernel, groups, heads),
        out_shape=[out] * 2,
        name="unpack",
    )(*received)


def local(queries, key_rows, value_rows, cotangent, lengths):
    rows = queries.shape[0]
    groups = key_rows.shape[1] // HD
    heads = queries.shape[1] // HD // groups
    shares = lax.axis_size("head")
    ctx = lax.axis_index("ctx")
    odd = lax.rem(ctx, 2) == 1
    ctx_in = ctx.astype(jnp.int32).reshape(1)

    def exchanged(value):
        return lax.all_to_all(value.reshape(shares, rows // shares, -1), "head",
                              split_axis=0, concat_axis=0, tiled=True)

    def hop_sum(back, parts):
        back_4, back_a, back_b = (x.astype(jnp.float32) for x in back)
        own, d2 = parts
        mid = d2.astype(jnp.float32) + back_b + back_4 + jnp.where(odd, back_a, 0.0)
        return own, back[1], shifted(mid.astype(jnp.bfloat16), -2)

    gathered = []
    for group in range(groups):
        cols = slice(group * HD, (group + 1) * HD)
        own = jnp.concatenate([key_rows[:, cols], value_rows[:, cols]], axis=1)
        count = lax.axis_size("ctx")
        r2 = shifted(own, 2)
        near = lax.ppermute(own, "ctx", [(i, i + 1) for i in range(0, count, 2)])
        r4 = shifted(r2, 2)
        b = swapped(r2)
        a = lax.ppermute(r2, "ctx", [(i, i + 1) for i in range(1, count - 1, 2)])
        gathered.append((own, near, r2, r4, b, a))

    tie = lax.optimization_barrier
    received, sums, moving = [], [], None
    for group in range(groups):
        produced = attend(lengths, ctx_in, queries, cotangent, gathered[group], group, heads)
        if group:
            (out, back), produced = tie(((exchanged(moving[0]), moving[1]), produced))
            received.append(out)
            sums.append(hop_sum(back, moving[2]))
        out, down, d2, d4, db, da = produced
        back = (shifted(d4, -2), shifted(da, -1), swapped(db))
        moving = (out, back, (down, d2))
    out, back, parts = moving
    out, swapped_back = tie((out, back[2]))
    received.append(exchanged(out))
    sums.append(hop_sum(back[:2] + (swapped_back,), parts))

    grads = [(own + back_2.astype(jnp.float32) + jnp.where(odd, 0.0, back_a.astype(jnp.float32))).astype(jnp.bfloat16)
             for own, back_a, back_2 in sums]
    grads = exchanged(jnp.concatenate(grads, axis=1))
    attention, query_grad = unpacked(received, heads)
    attention, query_grad, grads = tie((attention, query_grad, grads))
    key_grad, value_grad = unpacked([grads], groups)
    return attention, query_grad, key_grad, value_grad


def solution(mesh):
    return jax.shard_map(
        local,
        mesh=mesh,
        in_specs=(P("ctx", "head"), P("ctx", "head"), P("ctx", "head"), P("ctx", "head"), P()),
        out_specs=(P(("ctx", "head"), None),) * 4,
        check_vma=False,
    )
```

```python
import functools

import jax
import jax.numpy as jnp
from jax import lax
from jax.experimental import pallas as pl
from jax.experimental.pallas import tpu as pltpu
from jax.sharding import PartitionSpec as P

HD = 128
REACH = 4
LOG2E = 1.4426950408889634
MASKED = -1e30
VMEM_LIMIT = 40


def shifted(value, steps):
    count = lax.axis_size("ctx")
    first, last = max(0, -steps), min(count, count - steps)
    return lax.ppermute(value, "ctx", [(i, i + steps) for i in range(first, last)])


def swapped(value):
    return lax.ppermute(value, "ctx", [(i, i ^ 1) for i in range(lax.axis_size("ctx"))])


def over_rows(a, b):
    return lax.dot_general(a, b, (((0,), (0,)), ((), ())), preferred_element_type=jnp.float32)


def attend_kernel(tq, tk, heads, len_ref, ctx_ref, q_ref, g_ref, own_ref, near_ref, r2_ref, r4_ref, b_ref, a_ref,
                  out_ref, down_ref, d2_ref, d4_ref, db_ref, da_ref,
                  k_scr, v_scr, p_scr, acc_scr, top_scr, s_scr):
    rows = own_ref.shape[0]
    width = heads * tq
    step_q = pl.program_id(0)
    ctx = ctx_ref[0]
    odd = lax.rem(ctx, 2)
    base = ctx * rows
    kbase = base - REACH * rows
    docs = len_ref.shape[0]
    scale = HD ** -0.5
    bf16 = jnp.bfloat16

    def start_of(pos, zero):
        def body(d, carry):
            run, best = carry
            return run + len_ref[d], jnp.where(run <= pos, run, best)
        return lax.fori_loop(0, docs, body, (jnp.int32(0), zero))[1]

    slot_b, slot_a = 3 - 2 * odd, 1 + 2 * odd

    @pl.when(step_q == 0)
    def _():
        def place(ref, slot):
            at = pl.ds(pl.multiple_of(tk + slot * rows, rows), rows)
            k_scr[at, :] = ref[:, :HD]
            v_scr[at, :] = ref[:, HD:]

        for ref, slot in ((r4_ref, 0), (r2_ref, 2), (own_ref, 4), (b_ref, slot_b)):
            place(ref, slot)
        pl.when(odd == 1)(lambda: place(near_ref, 3))
        pl.when(odd == 0)(lambda: place(a_ref, 1))
        k_scr[:tk, :] = jnp.zeros((tk, HD), bf16)
        v_scr[:tk, :] = jnp.zeros((tk, HD), bf16)
        acc_scr[...] = jnp.zeros_like(acc_scr)

    q0 = step_q * tq
    end = REACH * rows + q0 + tq
    first = jnp.maximum(start_of(base + q0, jnp.int32(0)) - kbase, 0)
    last = jnp.maximum(start_of(base + q0 + tq - 1, jnp.int32(0)) - kbase, 0)
    tiles = (end - first + tk - 1) // tk
    whole = jnp.clip((end - last) // tk, 1, tiles)

    q = jnp.concatenate([q_ref[:, h * HD:(h + 1) * HD] for h in range(heads)], axis=0)
    g = jnp.concatenate([g_ref[:, h * HD:(h + 1) * HD] for h in range(heads)], axis=0)
    q_t, g_t = q.T, g.T
    q_pos = base + q0 + lax.rem(lax.broadcasted_iota(jnp.int32, (8, width), 1), tq)
    starts = start_of(q_pos, jnp.zeros((8, width), jnp.int32))[0:1, :]
    span = q_pos[0:1, :] - starts
    key_iota = lax.broadcasted_iota(jnp.int32, (tk, width), 0)

    def tile(t):
        return pl.ds(pl.multiple_of(tk + end - (t + 1) * tk, HD), tk)

    def scores(t, masked):
        s = jnp.dot(k_scr[tile(t), :], q_t, preferred_element_type=jnp.float32) * (scale * LOG2E)
        if masked:
            before = starts - (kbase + end - (t + 1) * tk)
            inside = key_iota >= before
            if masked == "both":
                inside &= key_iota <= before + span
            s = jnp.where(inside, s, MASKED)
        return s

    def top_of(top, s):
        return jnp.maximum(top, jnp.max(s, axis=0, keepdims=True))

    def weigh(t, before, top, total, acc, s):
        p = jnp.exp2(s - top)
        p_scr[tile(t), :] = p
        top_scr[t] = jnp.broadcast_to(top, (8, width))
        fade = jnp.exp2(before - top)
        total = total * fade + jnp.sum(p.reshape(tk // 8, 8, width), axis=0)
        return total, acc * fade + over_rows(v_scr[tile(t), :], p.astype(bf16))

    def forward(masked, t, carry):
        before, top, total, acc = carry
        s = s_scr[...]
        following = scores(t + 1, masked)
        new_top = top_of(top, following)
        total, acc = weigh(t, before, top, total, acc, s)
        s_scr[...] = following
        return top, new_top, total, acc

    s = scores(0, "both")
    top = top_of(jnp.full((1, width), MASKED, jnp.float32), s)
    s_scr[...] = s
    carry = (top, top, jnp.zeros((8, width), jnp.float32), jnp.zeros((HD, width), jnp.float32))
    carry = lax.fori_loop(0, whole - 1, functools.partial(forward, False), carry)
    before, top, total, acc = lax.fori_loop(whole - 1, tiles - 1, functools.partial(forward, True), carry)
    total, acc = weigh(tiles - 1, before, top, total, acc, s_scr[...])
    inverse = 1.0 / jnp.sum(total, axis=0, keepdims=True)
    attn_t = (acc * inverse).astype(bf16)
    delta = jnp.sum(attn_t.astype(jnp.float32) * g_t.astype(jnp.float32), axis=0, keepdims=True)

    def backward(t, dq):
        p = p_scr[tile(t), :] * (jnp.exp2(top_scr[t][0:1, :] - top) * inverse)
        dp = jnp.dot(v_scr[tile(t), :], g_t, preferred_element_type=jnp.float32)
        ds = (p * (dp - delta)).astype(bf16)
        acc_scr[tile(t), HD:] += jnp.dot(p.astype(bf16), g, preferred_element_type=jnp.float32)
        acc_scr[tile(t), :HD] += jnp.dot(ds, q, preferred_element_type=jnp.float32)
        return dq + over_rows(k_scr[tile(t), :], ds)

    dq_t = lax.fori_loop(0, tiles, backward, jnp.zeros((HD, width), jnp.float32))
    attn, dq = attn_t.T, (dq_t * scale).astype(bf16).T
    for h in range(heads):
        out_ref[:, 2 * h * HD:(2 * h + 1) * HD] = attn[h * tq:(h + 1) * tq, :]
        out_ref[:, (2 * h + 1) * HD:(2 * h + 2) * HD] = dq[h * tq:(h + 1) * tq, :]

    @pl.when(step_q == pl.num_programs(0) - 1)
    def _():
        for ref, slot in ((d4_ref, 0), (d2_ref, 2), (down_ref, 4), (db_ref, slot_b), (da_ref, slot_a)):
            at = pl.ds(pl.multiple_of(tk + slot * rows, rows), rows)
            ref[:, :HD] = (acc_scr[at, :HD] * scale).astype(ref.dtype)
            ref[:, HD:] = acc_scr[at, HD:].astype(ref.dtype)


def attend(lengths, ctx, queries, cotangent, blocks, group, heads):
    rows = queries.shape[0]
    tq, tk = min(256, rows), rows
    window = (REACH + 1) * rows
    whole = pl.BlockSpec((rows, 2 * HD), lambda t: (0, 0))
    smem = pl.BlockSpec(memory_space=pltpu.SMEM)
    columns = pl.BlockSpec((tq, heads * HD), lambda t: (t, group))
    block = jax.ShapeDtypeStruct((rows, 2 * HD), jnp.bfloat16)
    queries, cotangent, *blocks = (
        pltpu.with_memory_space_constraint(x, pltpu.HBM) for x in (queries, cotangent, *blocks))
    return pl.pallas_call(
        functools.partial(attend_kernel, tq, tk, heads),
        grid=(rows // tq,),
        in_specs=[smem, smem, columns, columns] + [whole] * 6,
        out_specs=[pl.BlockSpec((tq, heads * 2 * HD), lambda t: (t, 0))] + [whole] * 5,
        out_shape=[jax.ShapeDtypeStruct((rows, heads * 2 * HD), jnp.bfloat16),
                   block] + [block] * 4,
        scratch_shapes=[
            pltpu.VMEM((window + tk, HD), jnp.bfloat16),
            pltpu.VMEM((window + tk, HD), jnp.bfloat16),
            pltpu.VMEM((window + tk, heads * tq), jnp.float32),
            pltpu.VMEM((window + tk, 2 * HD), jnp.float32),
            pltpu.VMEM((window // tk + 1, 8, heads * tq), jnp.float32),
            pltpu.VMEM((tk, heads * tq), jnp.float32),
        ],
        compiler_params=pltpu.CompilerParams(vmem_limit_bytes=VMEM_LIMIT * 1024 * 1024),
        cost_estimate=pl.CostEstimate(
            flops=12 * heads * rows * window * HD, bytes_accessed=8 * 1024 * 1024,
            transcendentals=heads * rows * window),
        name="attend",
    )(lengths, ctx, queries, cotangent, *blocks)


def unpack_kernel(groups, heads, *refs):
    first_ref, second_ref = refs[groups:]
    shares = refs[0].shape[0]
    for share in range(shares):
        for group in range(groups):
            for head in range(heads):
                column = ((share * groups + group) * heads + head) * HD
                source = 2 * head * HD
                first_ref[:, column:column + HD] = refs[group][share, :, source:source + HD]
                second_ref[:, column:column + HD] = refs[group][share, :, source + HD:source + 2 * HD]


def unpacked(received, heads):
    groups = len(received)
    shares, part, _ = received[0].shape
    out = jax.ShapeDtypeStruct((part, shares * groups * heads * HD), jnp.bfloat16)
    return pl.pallas_call(
        functools.partial(unpack_kernel, groups, heads),
        out_shape=[out] * 2,
        name="unpack",
    )(*received)


def local(queries, key_rows, value_rows, cotangent, lengths):
    rows = queries.shape[0]
    groups = key_rows.shape[1] // HD
    heads = queries.shape[1] // HD // groups
    shares = lax.axis_size("head")
    ctx = lax.axis_index("ctx")
    odd = lax.rem(ctx, 2) == 1
    ctx_in = ctx.astype(jnp.int32).reshape(1)

    def exchanged(value):
        return lax.all_to_all(value.reshape(shares, rows // shares, -1), "head",
                              split_axis=0, concat_axis=0, tiled=True)

    def hop_sum(back, parts):
        back_4, back_a, back_b = (x.astype(jnp.float32) for x in back)
        own, d2 = parts
        mid = d2.astype(jnp.float32) + back_b + back_4 + jnp.where(odd, back_a, 0.0)
        return own, back[1], shifted(mid.astype(jnp.bfloat16), -2)

    gathered = []
    for group in range(groups):
        cols = slice(group * HD, (group + 1) * HD)
        own = jnp.concatenate([key_rows[:, cols], value_rows[:, cols]], axis=1)
        count = lax.axis_size("ctx")
        r2 = shifted(own, 2)
        near = lax.ppermute(own, "ctx", [(i, i + 1) for i in range(0, count, 2)])
        r4 = shifted(r2, 2)
        b = swapped(r2)
        a = lax.ppermute(r2, "ctx", [(i, i + 1) for i in range(1, count - 1, 2)])
        gathered.append((own, near, r2, r4, b, a))

    tie = lax.optimization_barrier
    received, sums, moving = [], [], None
    for group in range(groups):
        produced = attend(lengths, ctx_in, queries, cotangent, gathered[group], group, heads)
        if group:
            (out, back), produced = tie(((exchanged(moving[0]), moving[1]), produced))
            received.append(out)
            sums.append(hop_sum(back, moving[2]))
        out, down, d2, d4, db, da = produced
        back = (shifted(d4, -2), shifted(da, -1), swapped(db))
        moving = (out, back, (down, d2))
    out, back, parts = moving
    out, swapped_back = tie((out, back[2]))
    received.append(exchanged(out))
    sums.append(hop_sum(back[:2] + (swapped_back,), parts))

    grads = [(own.astype(jnp.float32) + back_2.astype(jnp.float32) + jnp.where(odd, 0.0, back_a.astype(jnp.float32))).astype(jnp.bfloat16)
             for own, back_a, back_2 in sums]
    grads = exchanged(jnp.concatenate(grads, axis=1))
    attention, query_grad = unpacked(received, heads)
    attention, query_grad, grads = tie((attention, query_grad, grads))
    key_grad, value_grad = unpacked([grads], groups)
    return attention, query_grad, key_grad, value_grad


def solution(mesh):
    return jax.shard_map(
        local,
        mesh=mesh,
        in_specs=(P("ctx", "head"), P("ctx", "head"), P("ctx", "head"), P("ctx", "head"), P()),
        out_specs=(P(("ctx", "head"), None),) * 4,
        check_vma=False,
    )
```
